32 devices in a mesh: dp: 16 (over z, x, core), seq: 2 (over y).
Axes of the slice: x: 2, y: 2, z: 4, core: 2. Of those that a mesh axis runs over, the one named last changes fastest.
Arguments:
- tokens: bfloat16 [8192, 1024], P(('dp', 'seq')), may hold values from -8 to 8
- segment_ids: int32 [16, 512], P('dp'), may hold values from 0 to 15, never falling along the last dimension, each value on 1 to 128 neighbouring positions
- cotangent: bfloat16 [8192, 1024], P(('dp', 'seq')), may hold values from -6 to 6
- gain_one: bfloat16 [1024], P(('dp', 'seq')), may hold values from 0.099609375 to 1.8984375
- gain_two: bfloat16 [1024], P(('dp', 'seq')), may hold values from 0.099609375 to 1.8984375
- conv_taps: bfloat16 [1024, 3], P(('dp', 'seq')), may hold values from -3 to 3
- w_in: bfloat16 [1024, 3072], P(('dp', 'seq')), may hold values from -0.1875 to 0.1875
- w_out: bfloat16 [1024, 1024], P(('dp', 'seq')), may hold values from -0.1875 to 0.1875
- w_gate: bfloat16 [1024, 4608], P(('dp', 'seq')), may hold values from -0.1875 to 0.1875
- w_up: bfloat16 [1024, 4608], P(('dp', 'seq')), may hold values from -0.1875 to 0.1875
- w_down: bfloat16 [1024, 4608], P(('dp', 'seq')), may hold values from -0.09375 to 0.09375
Outputs:
- block_out: bfloat16 [8192, 1024], P(('dp', 'seq'))
- grad_tokens: float32 [8192, 1024], P(('dp', 'seq'))
- grad_gain_one: float32 [1024], P(('dp', 'seq'))
- grad_gain_two: float32 [1024], P(('dp', 'seq'))
- grad_conv_taps: float32 [1024, 3], P(('dp', 'seq'))
- grad_in: float32 [1024, 3072], P(('dp', 'seq'))
- grad_out: float32 [1024, 1024], P(('dp', 'seq'))
- grad_gate: float32 [1024, 4608], P(('dp', 'seq'))
- grad_up: float32 [1024, 4608], P(('dp', 'seq'))
- grad_down: float32 [1024, 4608], P(('dp', 'seq'))
The draws below stay inside these ranges and needn't reach their ends.
Inputs may be any that keep to these rules, and one draw needn't show every extreme that they name: `segment_ids`: along each sequence the document numbers never fall; each document covers 1 to 128 positions in a row.
All inputs are finite; a program needn't handle non-finite values.
Results may differ from the reference program's by a relative error of at most 0.0093.
Values may be sent and summed in bfloat16 or wider, within the bound.
A program may use at most 256 MiB of HBM per device.

```python
import math
import jax
import jax.numpy as jnp
import numpy as np
from jax import lax

D = 1024
FF = 4608
TAPS = 3
SEQ_LEN = 512
SEQS = 16
TOKENS = 8192
SEG_COUNT = 16
SEG_MOST = 128


def draw_tokens(key, part):
    first = jax.random.fold_in(key, 11)
    second = jax.random.fold_in(key, 12)
    third = jax.random.fold_in(key, 13)
    base = jax.random.normal(first, (TOKENS, D), jnp.float32)
    column_scale = jnp.exp(jax.random.uniform(second, (1, D), jnp.float32, -1.15, 1.15))
    row_scale = jnp.exp(jax.random.uniform(third, (TOKENS, 1), jnp.float32, -0.7, 0.7))
    return jnp.clip(base * column_scale * row_scale, -8.0, 8.0).astype(jnp.bfloat16)


def levels(own_key, extent, split, smallest, top_value):
    def one(position, parts):
        steps = jax.random.uniform(jax.random.fold_in(jax.random.fold_in(own_key, 6), position), (parts,), jnp.float32, smallest / len(split), top_value / len(split))
        return jnp.repeat(jnp.exp(steps), extent[position] // parts).reshape((-1,) + (1,) * (len(extent) - position - 1))

    loudness = one(*split[0])
    for cut in split[1:]:
        loudness = loudness * one(*cut)
    return loudness


def profile(count, total, most, slope):
    portions = [(1 << 20) // math.isqrt(grade ** slope) + 1 for grade in range(2, count + 1)]
    spare, holding = total - most - (count - 1), [1] * (count - 1)
    while spare > 0:
        movable = [i for i in range(count - 1) if holding[i] < most]
        whole, budget = sum([portions[i] for i in movable]), spare
        for i in movable:
            more = min(most - holding[i], max(1, budget * portions[i] // whole), spare)
            holding[i] = holding[i] + more
            spare = spare - more
    return np.array([most] + holding)


def ragged_sizes(stream_key, amount, total, limit, skew):
    if amount == 2:
        one = jax.random.randint(stream_key, (), max(1, total - limit), min(limit, total - 1) + 1)
        return jnp.stack([one, total - one])
    lengths = jnp.asarray(profile(amount, total, limit, skew), jnp.int32)
    couples = (amount - 1) // 2
    giver, taker = lengths[1:1 + 2 * couples:2], lengths[2:2 + 2 * couples:2]
    slack = jnp.minimum(giver - 1, limit - taker)
    moved = jax.random.randint(jax.random.fold_in(stream_key, 1), (couples,), 0, 1 << 20) % (slack + 1)
    lengths = lengths.at[1:1 + 2 * couples:2].set(giver - moved).at[2:2 + 2 * couples:2].set(taker + moved)
    return lengths[jax.random.permutation(jax.random.fold_in(stream_key, 2), amount)]


def bell_draw(own_key, extent, deviation, reach, split=(), held_as=jnp.bfloat16):
    level = levels(own_key, extent, split, -0.22, 0.18) if split else 1.0
    entries = jax.random.normal(own_key, extent, jnp.float32) * deviation * level
    return jnp.minimum(jnp.maximum(entries, -reach), reach).astype(held_as)


def setup_inputs(seed: int = 0) -> dict:
    arg_keys = jax.random.split(jax.random.key(seed), 12)
    return {
        "tokens": draw_tokens(jax.random.fold_in(arg_keys[11], 71), 0),
        "segment_ids": jax.vmap(lambda own: jnp.searchsorted(jnp.cumsum(ragged_sizes(own, SEG_COUNT, SEQ_LEN, SEG_MOST, 1)), jnp.arange(SEQ_LEN), side="right"))(jax.random.split(arg_keys[1], SEQS)).reshape((SEQS, SEQ_LEN)).astype(jnp.int32),
        "cotangent": bell_draw(arg_keys[2], (TOKENS, D), 1.0, 6.0, ((0, 32),)),
        "gain_one": jnp.clip(1.0 + 0.18 * jax.random.normal(arg_keys[3], (D,), jnp.float32), 0.099609375, 1.8984375).astype(jnp.bfloat16),
        "gain_two": jnp.clip(1.0 + 0.18 * jax.random.normal(arg_keys[4], (D,), jnp.float32), 0.099609375, 1.8984375).astype(jnp.bfloat16),
        "conv_taps": bell_draw(arg_keys[5], (D, TAPS), 0.6, 3.0, ((0, 32),)),
        "w_in": bell_draw(arg_keys[6], (D, 3 * D), D ** -0.5, 0.1875, ((0, 32),)),
        "w_out": bell_draw(arg_keys[7], (D, D), D ** -0.5, 0.1875, ((0, 32),)),
        "w_gate": bell_draw(arg_keys[8], (D, FF), D ** -0.5, 0.1875, ((0, 32),)),
        "w_up": bell_draw(arg_keys[9], (D, FF), D ** -0.5, 0.1875, ((0, 32),)),
        "w_down": bell_draw(arg_keys[10], (D, FF), FF ** -0.5, 0.09375, ((0, 32),)),
    }


epsilon = 1e-06

def matmul(left, right):
    return jnp.dot(left, right, preferred_element_type=jnp.float32)

def matmul_tn(left, right):
    return lax.dot_general(left, right, (((0,), (0,)), ((), ())), preferred_element_type=jnp.float32)

def matmul_nt(left, right):
    return lax.dot_general(left, right, (((1,), (1,)), ((), ())), preferred_element_type=jnp.float32)

def mask_columns(padded_ids, offset, length):
    current = lax.dynamic_slice_in_dim(padded_ids, offset + 2, length)
    result = []
    for delay in range(3):
        earlier = lax.dynamic_slice_in_dim(padded_ids, offset + 2 - delay, length)
        result.append(jnp.where(jnp.logical_and(earlier == current, current >= 0), 1.0, 0.0).astype(jnp.float32)[:, None])
    return result

def norm_scale(values):
    return lax.rsqrt(lax.optimization_barrier(jnp.mean(values * values, axis=1, keepdims=True)) + epsilon)

def norm_backward(values, scale, gain_wide, grad):
    weighted = gain_wide * grad
    inner = lax.optimization_barrier(jnp.mean(weighted * values, axis=1, keepdims=True))
    back = scale * weighted - values * scale * scale * scale * inner
    return (back, lax.optimization_barrier(jnp.sum(grad * values * scale, axis=0)))

def front_part(token_rows, gain_one, w_in):
    rows_wide = token_rows.astype(jnp.float32)
    scale_one = norm_scale(rows_wide)
    normed_one = (rows_wide * scale_one * gain_one.astype(jnp.float32)).astype(jnp.bfloat16)
    projected = matmul(normed_one, w_in)
    features = projected.shape[1] // 3
    b_branch = projected[:, :features]
    c_branch = projected[:, features:2 * features]
    v_branch = projected[:, 2 * features:]
    return (rows_wide, scale_one, normed_one, b_branch, c_branch, v_branch, b_branch * v_branch)

def convolve(extended, masks, tap_weights):
    length = extended.shape[0] - 2
    summed = tap_weights[:, 2] * extended[2:2 + length] * masks[0]
    for delay in (1, 2):
        summed = summed + tap_weights[:, 2 - delay] * extended[2 - delay:2 - delay + length] * masks[delay]
    return summed

def back_convolve(back_ext, masks_ext, tap_weights):
    length = back_ext.shape[0] - 2
    summed = tap_weights[:, 2] * back_ext[:length] * masks_ext[0][:length]
    for delay in (1, 2):
        summed = summed + tap_weights[:, 2 - delay] * back_ext[delay:delay + length] * masks_ext[delay][delay:delay + length]
    return summed

def tap_gradient(back_conv, extended, masks):
    length = back_conv.shape[0]
    columns = []
    for column in range(3):
        delay = 2 - column
        columns.append(lax.optimization_barrier(jnp.sum(back_conv * extended[column:column + length] * masks[delay], axis=0)))
    return jnp.stack(columns, axis=1)

def tail_forward(rows_wide, c_branch, convolved, w_out, gain_two, w_gate, w_up, w_down):
    mixed_half = (c_branch * convolved).astype(jnp.bfloat16)
    residual = rows_wide + matmul(mixed_half, w_out)
    scale_two = norm_scale(residual)
    normed_two = (residual * scale_two * gain_two.astype(jnp.float32)).astype(jnp.bfloat16)
    gate_pre = matmul(normed_two, w_gate)
    up_proj = matmul(normed_two, w_up)
    hidden = (gate_pre * jax.nn.sigmoid(gate_pre) * up_proj).astype(jnp.bfloat16)
    block_out = (residual + matmul_nt(hidden, w_down)).astype(jnp.bfloat16)
    return (mixed_half, residual, scale_two, normed_two, gate_pre, up_proj, hidden, block_out)

def feed_backward(cotangent, normed_two, gate_pre, up_proj, hidden, residual, scale_two, gain_two, w_gate, w_up, w_down):
    back_hidden = matmul(cotangent, w_down)
    logistic = jax.nn.sigmoid(gate_pre)
    back_gate = (back_hidden * up_proj * logistic * (1.0 + gate_pre * (1.0 - logistic))).astype(jnp.bfloat16)
    back_up = (back_hidden * gate_pre * logistic).astype(jnp.bfloat16)
    grad_down = matmul_tn(cotangent, hidden)
    grad_gate = matmul_tn(normed_two, back_gate)
    grad_up = matmul_tn(normed_two, back_up)
    back_normed = matmul_nt(back_gate, w_gate) + matmul_nt(back_up, w_up)
    back_norm, grad_gain_two = norm_backward(residual, scale_two, gain_two.astype(jnp.float32), back_normed)
    back_residual = cotangent.astype(jnp.float32) + back_norm
    return (back_residual, grad_gain_two, grad_gate, grad_up, grad_down)

def one_sequence(token_rows, cot_rows, ids, gain_one, gain_two, conv_taps, w_in, w_out, w_gate, w_up, w_down):
    length = token_rows.shape[0]
    padded_ids = jnp.concatenate([jnp.full((2,), -1, jnp.int32), ids.astype(jnp.int32), jnp.full((2,), -2, jnp.int32)])
    tap_weights = conv_taps.astype(jnp.float32)
    rows_wide, scale_one, normed_one, b_branch, c_branch, v_branch, gated = front_part(token_rows, gain_one, w_in)
    rim = jnp.zeros((2, gated.shape[1]), jnp.float32)
    extended = jnp.concatenate([rim, gated], axis=0)
    masks = mask_columns(padded_ids, 0, length)
    convolved = convolve(extended, masks, tap_weights)
    mixed_half, residual, scale_two, normed_two, gate_pre, up_proj, hidden, block_out = tail_forward(rows_wide, c_branch, convolved, w_out, gain_two, w_gate, w_up, w_down)
    back_residual, grad_gain_two, grad_gate, grad_up, grad_down = feed_backward(cot_rows, normed_two, gate_pre, up_proj, hidden, residual, scale_two, gain_two, w_gate, w_up, w_down)
    back_out16 = back_residual.astype(jnp.bfloat16)
    grad_out = matmul_tn(mixed_half, back_out16)
    back_mixed = matmul_nt(back_out16, w_out)
    back_conv = back_mixed * c_branch
    back_c = back_mixed * convolved
    back_ext = jnp.concatenate([back_conv, rim], axis=0)
    masks_ext = mask_columns(padded_ids, 0, length + 2)
    back_gated = back_convolve(back_ext, masks_ext, tap_weights)
    grad_taps = tap_gradient(back_conv, extended, masks)
    back_proj = jnp.concatenate([back_gated * v_branch, back_c, back_gated * b_branch], axis=1).astype(jnp.bfloat16)
    grad_in = matmul_tn(normed_one, back_proj)
    back_normed_one = matmul_nt(back_proj, w_in)
    back_front, grad_gain_one = norm_backward(rows_wide, scale_one, gain_one.astype(jnp.float32), back_normed_one)
    grad_tokens = back_residual + back_front
    grads = (grad_gain_one, grad_gain_two, grad_taps, grad_in, grad_out, grad_gate, grad_up, grad_down)
    return (block_out, grad_tokens, grads)

def reference(tokens, segment_ids, cotangent, gain_one, gain_two, conv_taps, w_in, w_out, w_gate, w_up, w_down):
    token_seqs = tokens.reshape(SEQS, SEQ_LEN, D)
    cot_seqs = cotangent.reshape(SEQS, SEQ_LEN, D)
    init = (jnp.zeros((D,), jnp.float32), jnp.zeros((D,), jnp.float32), jnp.zeros((D, 3), jnp.float32), jnp.zeros((D, 3 * D), jnp.float32), jnp.zeros((D, D), jnp.float32), jnp.zeros((D, FF), jnp.float32), jnp.zeros((D, FF), jnp.float32), jnp.zeros((D, FF), jnp.float32))

    def advance(totals, element):
        token_rows, cot_rows, ids = element
        block_out, grad_tokens, grads = one_sequence(token_rows, cot_rows, ids, gain_one, gain_two, conv_taps, w_in, w_out, w_gate, w_up, w_down)
        return (tuple((left + right for left, right in zip(totals, grads))), (block_out, grad_tokens))
    totals, outputs = lax.scan(advance, init, (token_seqs, cot_seqs, segment_ids))
    block_out = outputs[0].reshape(TOKENS, D)
    grad_tokens = outputs[1].reshape(TOKENS, D)
    return (block_out, grad_tokens, totals[0], totals[1], totals[2], totals[3], totals[4], totals[5], totals[6], totals[7])
```

```python
import functools

import jax
import jax.numpy as jnp
from jax import lax
from jax.sharding import PartitionSpec as P

epsilon = 1e-06


def from_behind(shard, axis, by):
    devices = lax.axis_size(axis)
    pairs = [(i, i + by) for i in range(devices) if 0 <= i + by < devices]
    return lax.ppermute(shard, axis, pairs)


def matmul(left, right):
    return jnp.dot(left, right, preferred_element_type=jnp.float32)


def matmul_tn(left, right):
    return lax.dot_general(
        left, right, (((0,), (0,)), ((), ())), preferred_element_type=jnp.float32
    )


def matmul_nt(left, right):
    return lax.dot_general(
        left, right, (((1,), (1,)), ((), ())), preferred_element_type=jnp.float32
    )


def mask_columns(padded_ids, offset, length):
    current = lax.dynamic_slice_in_dim(padded_ids, offset + 2, length)
    result = []
    for delay in range(3):
        earlier = lax.dynamic_slice_in_dim(padded_ids, offset + 2 - delay, length)
        result.append(
            jnp.where(jnp.logical_and(earlier == current, current >= 0), 1.0, 0.0).astype(
                jnp.float32
            )[:, None]
        )
    return result


def norm_scale(values):
    return lax.rsqrt(jnp.mean(values * values, axis=1, keepdims=True) + epsilon)


def norm_backward(values, scale, gain_wide, grad):
    weighted = gain_wide * grad
    inner = jnp.mean(weighted * values, axis=1, keepdims=True)
    back = scale * weighted - values * scale * scale * scale * inner
    return (back, jnp.sum(grad * values * scale, axis=0))


def front_part(token_rows, gain_one, w_in):
    rows_wide = token_rows.astype(jnp.float32)
    scale_one = norm_scale(rows_wide)
    normed_one = (rows_wide * scale_one * gain_one.astype(jnp.float32)).astype(jnp.bfloat16)
    projected = matmul(normed_one, w_in)
    features = projected.shape[1] // 3
    b_branch = projected[:, :features]
    c_branch = projected[:, features : 2 * features]
    v_branch = projected[:, 2 * features :]
    return (rows_wide, scale_one, normed_one, b_branch, c_branch, v_branch, b_branch * v_branch)


def convolve(extended, masks, tap_weights):
    length = extended.shape[0] - 2
    summed = tap_weights[:, 2] * extended[2 : 2 + length] * masks[0]
    for delay in (1, 2):
        summed = (
            summed
            + tap_weights[:, 2 - delay] * extended[2 - delay : 2 - delay + length] * masks[delay]
        )
    return summed


def back_convolve(back_ext, masks_ext, tap_weights):
    length = back_ext.shape[0] - 2
    summed = tap_weights[:, 2] * back_ext[:length] * masks_ext[0][:length]
    for delay in (1, 2):
        summed = (
            summed
            + tap_weights[:, 2 - delay]
            * back_ext[delay : delay + length]
            * masks_ext[delay][delay : delay + length]
        )
    return summed


def tap_gradient(back_conv, extended, masks):
    length = back_conv.shape[0]
    columns = []
    for column in range(3):
        delay = 2 - column
        columns.append(
            jnp.sum(back_conv * extended[column : column + length] * masks[delay], axis=0)
        )
    return jnp.stack(columns, axis=1)


def tail_forward(rows_wide, c_branch, convolved, w_out, gain_two, w_gate, w_up, w_down):
    mixed_half = (c_branch * convolved).astype(jnp.bfloat16)
    residual = rows_wide + matmul(mixed_half, w_out)
    scale_two = norm_scale(residual)
    normed_two = (residual * scale_two * gain_two.astype(jnp.float32)).astype(jnp.bfloat16)
    gate_pre = matmul(normed_two, w_gate)
    up_proj = matmul(normed_two, w_up)
    hidden = (gate_pre * jax.nn.sigmoid(gate_pre) * up_proj).astype(jnp.bfloat16)
    block_out = (residual + matmul_nt(hidden, w_down)).astype(jnp.bfloat16)
    return (mixed_half, residual, scale_two, normed_two, gate_pre, up_proj, hidden, block_out)


def feed_backward(
    cotangent,
    normed_two,
    gate_pre,
    up_proj,
    hidden,
    residual,
    scale_two,
    gain_two,
    w_gate,
    w_up,
    w_down,
):
    back_hidden = matmul(cotangent, w_down)
    logistic = jax.nn.sigmoid(gate_pre)
    back_gate = (back_hidden * up_proj * logistic * (1.0 + gate_pre * (1.0 - logistic))).astype(
        jnp.bfloat16
    )
    back_up = (back_hidden * gate_pre * logistic).astype(jnp.bfloat16)
    grad_down = matmul_tn(cotangent, hidden)
    grad_gate = matmul_tn(normed_two, back_gate)
    grad_up = matmul_tn(normed_two, back_up)
    back_normed = matmul_nt(back_gate, w_gate) + matmul_nt(back_up, w_up)
    back_norm, grad_gain_two = norm_backward(
        residual, scale_two, gain_two.astype(jnp.float32), back_normed
    )
    back_residual = cotangent.astype(jnp.float32) + back_norm
    return (back_residual, grad_gain_two, grad_gate, grad_up, grad_down)


def levels(devices):
    return devices.bit_length() - 1


def cube(mesh_shape):
    dims = []
    for axis in ("dp", "seq"):
        count = levels(mesh_shape[axis])
        dims += [(axis, count - 1 - i) for i in range(count)]
    return dims


def orders(mesh_shape):
    near = levels(mesh_shape["dp"])
    far = levels(mesh_shape["seq"])
    inner = [near - 1]
    ring = [near - 2] if near > 1 else []
    outer = list(range(near, near + far))
    rest = list(range(near - 3, -1, -1))
    return (inner + ring + outer + rest, inner + outer + ring + rest)


def swap(shard, axis, bit):
    devices = lax.axis_size(axis)
    return lax.ppermute(shard, axis, [(i, i ^ (1 << bit)) for i in range(devices)])


def side_of(axis, bit):
    return (lax.axis_index(axis) >> bit) & 1


def scatter_sum(partial, order, dims):
    count = len(dims)
    held = partial.reshape((2,) * count + (partial.shape[0] >> count, partial.shape[1]))
    for step, dim in enumerate(order):
        axis, bit = dims[dim]
        side = side_of(axis, bit)
        mine = lax.dynamic_index_in_dim(held, side, dim, keepdims=True)
        theirs = lax.dynamic_index_in_dim(held, 1 - side, dim, keepdims=True)
        came = swap(theirs, axis, bit)
        held = mine.astype(jnp.float32) + came.astype(jnp.float32)
        if step + 1 < count:
            held = held.astype(jnp.bfloat16)
    return held.reshape(held.shape[count:])


def join(shard, dim, axis, bit):
    came = swap(shard, axis, bit)
    low = jnp.where(side_of(axis, bit) == 0, shard, came)
    high = jnp.where(side_of(axis, bit) == 0, came, shard)
    return jnp.concatenate([low, high], axis=dim)


def gather_rows(shard, order, dims):
    count = len(dims)
    held = shard.reshape((1,) * count + shard.shape)
    for dim in reversed(order):
        axis, bit = dims[dim]
        held = join(held, dim, axis, bit)
    return held.reshape((shard.shape[0] << count, shard.shape[1]))


def cut(columns):
    return (columns // 256) * 128


def gather_pair(shard, both, dims):
    count = len(dims)
    at = cut(shard.shape[1])
    parts = []
    for piece, order in ((shard[:, :at], both[0]), (shard[:, at:], both[1])):
        held = piece.reshape((1,) * count + piece.shape)
        for dim in reversed(order[1:]):
            axis, bit = dims[dim]
            held = join(held, dim, axis, bit)
        parts.append(held)
    held = jnp.concatenate(parts, axis=count + 1)
    axis, bit = dims[both[0][0]]
    held = join(held, both[0][0], axis, bit)
    return held.reshape((shard.shape[0] << count, shard.shape[1]))


def scatter_pair(partial, both, dims):
    at = cut(partial.shape[1])
    small = partial.astype(jnp.bfloat16)
    return jnp.concatenate(
        [
            scatter_sum(small[:, :at], both[0], dims),
            scatter_sum(small[:, at:], both[1], dims),
        ],
        axis=1,
    )


def body_whole(
    dims,
    both,
    tokens,
    segment_ids,
    cotangent,
    gain_one,
    gain_two,
    conv_taps,
    w_in,
    w_out,
    w_gate,
    w_up,
    w_down,
):
    taps = conv_taps.shape[1]
    small = jnp.concatenate([gain_one[:, None], gain_two[:, None], conv_taps], axis=1)
    small = jnp.pad(small, ((0, 0), (0, 128 - small.shape[1])))
    first = gather_pair(jnp.concatenate([small, w_in], axis=1), both, dims)
    full_g_one, full_g_two, full_taps = first[:, 0], first[:, 1], first[:, 2 : 2 + taps]
    full_in = first[:, 128:]
    full_out = gather_pair(w_out, both, dims)
    full_gate = gather_pair(w_gate, both, dims)
    full_up = gather_pair(w_up, both, dims)
    full_down = gather_pair(w_down, both, dims)
    length = tokens.shape[0]
    offset = lax.axis_index("seq") * length
    padded_ids = jnp.concatenate(
        [jnp.full((2,), -1, jnp.int32), segment_ids[0], jnp.full((2,), -2, jnp.int32)]
    )
    tap_weights = full_taps.astype(jnp.float32)
    rows_wide, scale_one, normed_one, b_branch, c_branch, v_branch, gated = front_part(
        tokens, full_g_one, full_in
    )
    before = from_behind(gated[length - 2 :], "seq", 1)
    extended = jnp.concatenate([before, gated], axis=0)
    masks = mask_columns(padded_ids, offset, length)
    convolved = convolve(extended, masks, tap_weights)
    mixed_half, residual, scale_two, normed_two, gate_pre, up_proj, hidden, block_out = (
        tail_forward(
            rows_wide, c_branch, convolved, full_out, full_g_two, full_gate, full_up, full_down
        )
    )
    back_residual, grad_gain_two, grad_gate, grad_up, grad_down = feed_backward(
        cotangent,
        normed_two,
        gate_pre,
        up_proj,
        hidden,
        residual,
        scale_two,
        full_g_two,
        full_gate,
        full_up,
        full_down,
    )
    sum_down = scatter_pair(grad_down, both, dims)
    sum_gate = scatter_pair(grad_gate, both, dims)
    sum_up = scatter_pair(grad_up, both, dims)
    back_out16 = back_residual.astype(jnp.bfloat16)
    grad_out = matmul_tn(mixed_half, back_out16)
    back_mixed = matmul_nt(back_out16, full_out)
    back_conv = back_mixed * c_branch
    back_c = back_mixed * convolved
    after = from_behind(back_conv[:2], "seq", -1)
    back_ext = jnp.concatenate([back_conv, after], axis=0)
    masks_ext = mask_columns(padded_ids, offset, length + 2)
    back_gated = back_convolve(back_ext, masks_ext, tap_weights)
    grad_taps = tap_gradient(back_conv, extended, masks)
    back_proj = jnp.concatenate(
        [back_gated * v_branch, back_c, back_gated * b_branch], axis=1
    ).astype(jnp.bfloat16)
    grad_in = matmul_tn(normed_one, back_proj)
    back_normed_one = matmul_nt(back_proj, full_in)
    back_front, grad_gain_one = norm_backward(
        rows_wide, scale_one, full_g_one.astype(jnp.float32), back_normed_one
    )
    grad_tokens = back_residual + back_front
    grads_small = jnp.concatenate(
        [grad_gain_one[:, None], grad_gain_two[:, None], grad_taps], axis=1
    )
    grads_small = jnp.pad(grads_small, ((0, 0), (0, 128 - grads_small.shape[1])))
    sum_in = scatter_pair(grad_in, both, dims)
    sum_rest = scatter_pair(jnp.concatenate([grads_small, grad_out], axis=1), both, dims)
    return (
        block_out,
        grad_tokens,
        sum_rest[:, 0],
        sum_rest[:, 1],
        sum_rest[:, 2 : 2 + taps],
        sum_in,
        sum_rest[:, 128:],
        sum_gate,
        sum_up,
        sum_down,
    )


def solution(mesh):
    in_specs = (
        P(("dp", "seq"), None),
        P("dp", None),
        P(("dp", "seq"), None),
        P(("dp", "seq")),
        P(("dp", "seq")),
        P(("dp", "seq"), None),
        P(("dp", "seq"), None),
        P(("dp", "seq"), None),
        P(("dp", "seq"), None),
        P(("dp", "seq"), None),
        P(("dp", "seq"), None),
    )
    out_specs = (
        P(("dp", "seq"), None),
        P(("dp", "seq"), None),
        P(("dp", "seq")),
        P(("dp", "seq")),
        P(("dp", "seq"), None),
        P(("dp", "seq"), None),
        P(("dp", "seq"), None),
        P(("dp", "seq"), None),
        P(("dp", "seq"), None),
        P(("dp", "seq"), None),
    )
    body = functools.partial(body_whole, cube(mesh.shape), orders(mesh.shape))
    return jax.shard_map(body, mesh=mesh, in_specs=in_specs, out_specs=out_specs, check_vma=False)
```

```python
import functools

import jax
import jax.numpy as jnp
from jax import lax
from jax.sharding import PartitionSpec as P

epsilon = 1e-06


def from_behind(shard, axis, by):
    devices = lax.axis_size(axis)
    pairs = [(i, i + by) for i in range(devices) if 0 <= i + by < devices]
    return lax.ppermute(shard, axis, pairs)


def matmul(left, right):
    return jnp.dot(left, right, preferred_element_type=jnp.float32)


def matmul_tn(left, right):
    return lax.dot_general(
        left, right, (((0,), (0,)), ((), ())), preferred_element_type=jnp.float32
    )


def matmul_nt(left, right):
    return lax.dot_general(
        left, right, (((1,), (1,)), ((), ())), preferred_element_type=jnp.float32
    )


def mask_columns(padded_ids, offset, length):
    current = lax.dynamic_slice_in_dim(padded_ids, offset + 2, length)
    result = []
    for delay in range(3):
        earlier = lax.dynamic_slice_in_dim(padded_ids, offset + 2 - delay, length)
        result.append(
            jnp.where(jnp.logical_and(earlier == current, current >= 0), 1.0, 0.0).astype(
                jnp.float32
            )[:, None]
        )
    return result


def norm_scale(values):
    return lax.rsqrt(jnp.mean(values * values, axis=1, keepdims=True) + epsilon)


def norm_backward(values, scale, gain_wide, grad):
    weighted = gain_wide * grad
    inner = jnp.mean(weighted * values, axis=1, keepdims=True)
    back = scale * weighted - values * scale * scale * scale * inner
    return (back, jnp.sum(grad * values * scale, axis=0))


def front_part(token_rows, gain_one, w_in):
    rows_wide = token_rows.astype(jnp.float32)
    scale_one = norm_scale(rows_wide)
    normed_one = (rows_wide * scale_one * gain_one.astype(jnp.float32)).astype(jnp.bfloat16)
    projected = matmul(normed_one, w_in)
    features = projected.shape[1] // 3
    b_branch = projected[:, :features]
    c_branch = projected[:, features : 2 * features]
    v_branch = projected[:, 2 * features :]
    return (rows_wide, scale_one, normed_one, b_branch, c_branch, v_branch, b_branch * v_branch)


def convolve(extended, masks, tap_weights):
    length = extended.shape[0] - 2
    summed = tap_weights[:, 2] * extended[2 : 2 + length] * masks[0]
    for delay in (1, 2):
        summed = (
            summed
            + tap_weights[:, 2 - delay] * extended[2 - delay : 2 - delay + length] * masks[delay]
        )
    return summed


def back_convolve(back_ext, masks_ext, tap_weights):
    length = back_ext.shape[0] - 2
    summed = tap_weights[:, 2] * back_ext[:length] * masks_ext[0][:length]
    for delay in (1, 2):
        summed = (
            summed
            + tap_weights[:, 2 - delay]
            * back_ext[delay : delay + length]
            * masks_ext[delay][delay : delay + length]
        )
    return summed


def tap_gradient(back_conv, extended, masks):
    length = back_conv.shape[0]
    columns = []
    for column in range(3):
        delay = 2 - column
        columns.append(
            jnp.sum(back_conv * extended[column : column + length] * masks[delay], axis=0)
        )
    return jnp.stack(columns, axis=1)


def tail_forward(rows_wide, c_branch, convolved, w_out, gain_two, w_gate, w_up, w_down):
    mixed_half = (c_branch * convolved).astype(jnp.bfloat16)
    residual = rows_wide + matmul(mixed_half, w_out)
    scale_two = norm_scale(residual)
    normed_two = (residual * scale_two * gain_two.astype(jnp.float32)).astype(jnp.bfloat16)
    gate_pre = matmul(normed_two, w_gate)
    up_proj = matmul(normed_two, w_up)
    hidden = (gate_pre * jax.nn.sigmoid(gate_pre) * up_proj).astype(jnp.bfloat16)
    block_out = (residual + matmul_nt(hidden, w_down)).astype(jnp.bfloat16)
    return (mixed_half, residual, scale_two, normed_two, gate_pre, up_proj, hidden, block_out)


def feed_backward(
    cotangent,
    normed_two,
    gate_pre,
    up_proj,
    hidden,
    residual,
    scale_two,
    gain_two,
    w_gate,
    w_up,
    w_down,
):
    back_hidden = matmul(cotangent, w_down)
    logistic = jax.nn.sigmoid(gate_pre)
    back_gate = (back_hidden * up_proj * logistic * (1.0 + gate_pre * (1.0 - logistic))).astype(
        jnp.bfloat16
    )
    back_up = (back_hidden * gate_pre * logistic).astype(jnp.bfloat16)
    grad_down = matmul_tn(cotangent, hidden)
    grad_gate = matmul_tn(normed_two, back_gate)
    grad_up = matmul_tn(normed_two, back_up)
    back_normed = matmul_nt(back_gate, w_gate) + matmul_nt(back_up, w_up)
    back_norm, grad_gain_two = norm_backward(
        residual, scale_two, gain_two.astype(jnp.float32), back_normed
    )
    back_residual = cotangent.astype(jnp.float32) + back_norm
    return (back_residual, grad_gain_two, grad_gate, grad_up, grad_down)


def levels(devices):
    return devices.bit_length() - 1


def cube(mesh_shape):
    dims = []
    for axis in ("dp", "seq"):
        count = levels(mesh_shape[axis])
        dims += [(axis, count - 1 - i) for i in range(count)]
    return dims


def orders(mesh_shape):
    near = levels(mesh_shape["dp"])
    far = levels(mesh_shape["seq"])
    inner = [near - 1]
    ring = [near - 2] if near > 1 else []
    outer = list(range(near, near + far))
    rest = list(range(near - 3, -1, -1))
    return (inner + ring + outer + rest, inner + outer + ring + rest)


def swap(shard, axis, bit):
    devices = lax.axis_size(axis)
    return lax.ppermute(shard, axis, [(i, i ^ (1 << bit)) for i in range(devices)])


def side_of(axis, bit):
    return (lax.axis_index(axis) >> bit) & 1


def scatter_sum(partial, order, dims):
    count = len(dims)
    held = partial.reshape((2,) * count + (partial.shape[0] >> count, partial.shape[1]))
    for step, dim in enumerate(order):
        axis, bit = dims[dim]
        side = side_of(axis, bit)
        mine = lax.dynamic_index_in_dim(held, side, dim, keepdims=True)
        theirs = lax.dynamic_index_in_dim(held, 1 - side, dim, keepdims=True)
        came = swap(theirs, axis, bit)
        held = mine.astype(jnp.float32) + came.astype(jnp.float32)
        if step + 1 < count:
            held = held.astype(jnp.bfloat16)
    return held.reshape(held.shape[count:])


def join(shard, dim, axis, bit):
    came = swap(shard, axis, bit)
    wide = shard.shape[:dim] + (2,) + shard.shape[dim + 1 :]
    place = lax.broadcasted_iota(jnp.int32, wide, dim)
    return jnp.where(place == side_of(axis, bit), shard, came)


def cut(columns):
    return (columns // 256) * 128


def gather_pair(shard, both, dims):
    count = len(dims)
    at = cut(shard.shape[1])
    parts = []
    for piece, order in ((shard[:, :at], both[0]), (shard[:, at:], both[1])):
        held = piece.reshape((1,) * count + piece.shape)
        for dim in reversed(order[1:]):
            axis, bit = dims[dim]
            held = join(held, dim, axis, bit)
        parts.append(held)
    held = jnp.concatenate(parts, axis=count + 1)
    axis, bit = dims[both[0][0]]
    held = join(held, both[0][0], axis, bit)
    return held.reshape((shard.shape[0] << count, shard.shape[1]))


def scatter_pair(partial, both, dims):
    at = cut(partial.shape[1])
    small = partial.astype(jnp.bfloat16)
    return jnp.concatenate(
        [
            scatter_sum(small[:, :at], both[0], dims),
            scatter_sum(small[:, at:], both[1], dims),
        ],
        axis=1,
    )


def body_whole(
    dims,
    both,
    tokens,
    segment_ids,
    cotangent,
    gain_one,
    gain_two,
    conv_taps,
    w_in,
    w_out,
    w_gate,
    w_up,
    w_down,
):
    taps = conv_taps.shape[1]
    small = jnp.concatenate([gain_one[:, None], gain_two[:, None], conv_taps], axis=1)
    small = jnp.pad(small, ((0, 0), (0, 128 - small.shape[1])))
    first = gather_pair(jnp.concatenate([small, w_in, w_out], axis=1), both, dims)
    full_g_one, full_g_two, full_taps = first[:, 0], first[:, 1], first[:, 2 : 2 + taps]
    full_in = first[:, 128 : 128 + w_in.shape[1]]
    full_out = first[:, 128 + w_in.shape[1] :]
    full_gate = gather_pair(w_gate, both, dims)
    full_up = gather_pair(w_up, both, dims)
    full_down = gather_pair(w_down, both, dims)
    length = tokens.shape[0]
    offset = lax.axis_index("seq") * length
    padded_ids = jnp.concatenate(
        [jnp.full((2,), -1, jnp.int32), segment_ids[0], jnp.full((2,), -2, jnp.int32)]
    )
    tap_weights = full_taps.astype(jnp.float32)
    rows_wide, scale_one, normed_one, b_branch, c_branch, v_branch, gated = front_part(
        tokens, full_g_one, full_in
    )
    before = from_behind(gated[length - 2 :], "seq", 1)
    extended = jnp.concatenate([before, gated], axis=0)
    masks = mask_columns(padded_ids, offset, length)
    convolved = convolve(extended, masks, tap_weights)
    mixed_half, residual, scale_two, normed_two, gate_pre, up_proj, hidden, block_out = (
        tail_forward(
            rows_wide, c_branch, convolved, full_out, full_g_two, full_gate, full_up, full_down
        )
    )
    back_residual, grad_gain_two, grad_gate, grad_up, grad_down = feed_backward(
        cotangent,
        normed_two,
        gate_pre,
        up_proj,
        hidden,
        residual,
        scale_two,
        full_g_two,
        full_gate,
        full_up,
        full_down,
    )
    sum_down = scatter_pair(grad_down, both, dims)
    sum_gate = scatter_pair(grad_gate, both, dims)
    sum_up = scatter_pair(grad_up, both, dims)
    back_out16 = back_residual.astype(jnp.bfloat16)
    grad_out = matmul_tn(mixed_half, back_out16)
    back_mixed = matmul_nt(back_out16, full_out)
    back_conv = back_mixed * c_branch
    back_c = back_mixed * convolved
    after = from_behind(back_conv[:2], "seq", -1)
    back_ext = jnp.concatenate([back_conv, after], axis=0)
    masks_ext = mask_columns(padded_ids, offset, length + 2)
    back_gated = back_convolve(back_ext, masks_ext, tap_weights)
    grad_taps = tap_gradient(back_conv, extended, masks)
    back_proj = jnp.concatenate(
        [back_gated * v_branch, back_c, back_gated * b_branch], axis=1
    ).astype(jnp.bfloat16)
    grad_in = matmul_tn(normed_one, back_proj)
    back_normed_one = matmul_nt(back_proj, full_in)
    back_front, grad_gain_one = norm_backward(
        rows_wide, scale_one, full_g_one.astype(jnp.float32), back_normed_one
    )
    grad_tokens = back_residual + back_front
    grads_small = jnp.concatenate(
        [grad_gain_one[:, None], grad_gain_two[:, None], grad_taps], axis=1
    )
    grads_small = jnp.pad(grads_small, ((0, 0), (0, 128 - grads_small.shape[1])))
    packed = jnp.concatenate([grads_small, grad_out, grad_in], axis=1)
    sum_rest = scatter_pair(packed, both, dims)
    edge = 128 + grad_out.shape[1]
    return (
        block_out,
        grad_tokens,
        sum_rest[:, 0],
        sum_rest[:, 1],
        sum_rest[:, 2 : 2 + taps],
        sum_rest[:, edge:],
        sum_rest[:, 128:edge],
        sum_gate,
        sum_up,
        sum_down,
    )


def solution(mesh):
    in_specs = (
        P(("dp", "seq"), None),
        P("dp", None),
        P(("dp", "seq"), None),
        P(("dp", "seq")),
        P(("dp", "seq")),
        P(("dp", "seq"), None),
        P(("dp", "seq"), None),
        P(("dp", "seq"), None),
        P(("dp", "seq"), None),
        P(("dp", "seq"), None),
        P(("dp", "seq"), None),
    )
    out_specs = (
        P(("dp", "seq"), None),
        P(("dp", "seq"), None),
        P(("dp", "seq")),
        P(("dp", "seq")),
        P(("dp", "seq"), None),
        P(("dp", "seq"), None),
        P(("dp", "seq"), None),
        P(("dp", "seq"), None),
        P(("dp", "seq"), None),
        P(("dp", "seq"), None),
    )
    body = functools.partial(body_whole, cube(mesh.shape), orders(mesh.shape))
    return jax.shard_map(body, mesh=mesh, in_specs=in_specs, out_specs=out_specs, check_vma=False)
```
